32 devices in a mesh: cohort: 4 (over y, x), gene: 8 (over z, core).
Axes of the slice: x: 2, y: 2, z: 4, core: 2. Of those that a mesh axis runs over, the one named last changes fastest.
Arguments:
- scores: bfloat16 [4, 49152, 512], P('cohort', 'gene'), may hold values from -6 to 6
- flips: int32 [4, 49152], P('cohort', 'gene'), may hold values from 0 to 1
- presence: int32 [4, 49152], P('cohort', 'gene'), may hold values 0 or 1
- covs: bfloat16 [4, 384, 128, 128], P('cohort', 'gene'), may hold values from -2 to 2.5, as said below
- membership: int32 [8, 49152], P(None, 'gene'), may hold values 0 or 1
- weights: float32 [49152], P('gene'), may hold values from 0.25 to 4
- tile_owner: int32 [384, 1], P('gene'), may hold values from 0 to 7; in each aligned block of 48 rows (0 to 47, 48 to 95, ...) at most 12 rows name the same one
- tile_gene: int32 [384], P('gene'), may hold values from 0 to 15
Outputs:
- burden_z: float32 [128, 8, 512], P('gene', None, 'cohort')
- skat_z: float32 [128, 8, 512], P('gene', None, 'cohort')
The draws below stay inside these ranges and needn't reach their ends.
Inputs may be any that keep to these rules, and one draw needn't show every extreme that they name: `tile_owner`: in the tiles of one device (aligned blocks of 48 tiles) at most 12 belong to one owner. `covs`: each block is symmetric.
All inputs are finite; a program needn't handle non-finite values. No bound on the sum of `presence` or of `membership` on one device may be relied on, other than what follows from the above.
Results may differ from the reference program's by a relative error of at most 0.035.
Values may be sent and summed in bfloat16 or wider, within the bound.
No kernel may reach another device: no remote copies, remote signals or barrier semaphores. Data moves between devices by JAX's collectives and lax.ppermute only.
A program may use at most 128 MiB of HBM per device.

```python
import math
import jax
import jax.numpy as jnp
import numpy as np
from jax import lax

VT = 128
P_SIZE = 512
MASKS = 8
TILE_DEV = 48
GENE_DEV = 16
COHORTS = 4
TILES = 384
VARIANTS = 49152
GENES = 128
CAP = 12
N_GENE = 8


def flip_bits(key):
    return jax.random.randint(jax.random.fold_in(key, 101), (COHORTS, VARIANTS), 0, 2, dtype=jnp.int32)


def draw_flips(key, part):
    return flip_bits(key)


def draw_covs(key, part):
    base = jax.random.fold_in(key, 202)
    scale_key, nugget_key, length_key, rough_key = jax.random.split(base, 4)
    allele_sign = (1.0 - 2.0 * flip_bits(key).astype(jnp.float32)).reshape(COHORTS, TILES, VT)
    position = jnp.arange(VT, dtype=jnp.float32)
    distance = jnp.abs(position[:, None] - position[None, :])
    length = VT * jax.random.uniform(length_key, (COHORTS, TILES, 1, 1), jnp.float32, 0.06, 0.4)
    rough = jax.random.uniform(rough_key, (COHORTS, TILES, VT, VT), jnp.float32, 0.0, 0.6)
    rough = 0.5 * (rough + jnp.swapaxes(rough, 2, 3))
    scale = jax.random.uniform(scale_key, (COHORTS, TILES, VT), jnp.float32, 0.75, 1.25)
    nugget = jax.random.uniform(nugget_key, (COHORTS, TILES, VT), jnp.float32, 0.1, 0.4)
    envelope = jnp.exp(-distance / length)
    identity = jnp.eye(VT, dtype=jnp.float32)
    shared = envelope * (1.0 - rough) * (1.0 - identity) + identity * (1.0 + nugget[:, :, :, None])
    signed_scale = scale * allele_sign
    blocks = signed_scale[:, :, :, None] * signed_scale[:, :, None, :] * shared
    return blocks.astype(jnp.bfloat16)


def with_ends(result, own_key, smallest, top_value):
    longest = result.shape.index(max(result.shape))
    spots = []
    for shift in (0, 1):
        where = [jax.random.randint(jax.random.fold_in(own_key, axis), (), 0, length) for axis, length in enumerate(result.shape)]
        where[longest] = (where[longest] + shift) % result.shape[longest]
        spots.append(tuple(where))
    return result.at[spots[0]].set(smallest).at[spots[1]].set(top_value)


def shard_levels(stream_key, extent, cuts, low, high):
    def one(dim, blocks):
        heights = jax.random.uniform(jax.random.fold_in(jax.random.fold_in(stream_key, 6), dim), (blocks,), jnp.float32, low / len(cuts), high / len(cuts))
        return jnp.repeat(jnp.exp(heights), extent[dim] // blocks).reshape((-1,) + (1,) * (len(extent) - dim - 1))

    level = one(*cuts[0])
    for cut in cuts[1:]:
        level = level * one(*cut)
    return level


def shared_out(key, own, number, rows, number_of, top, most, skew):
    order = jax.random.permutation(key, number_of)
    crowded, ordinary = load_shares(number_of, rows * top, most, skew, True), load_shares(number_of, rows * top, most, skew, False)
    places = jnp.arange(number_of)

    def named(tallies, rotation):
        used = int((tallies > 0).sum())
        fixed = max(1, used // 4)
        shifted = fixed + (places - fixed + rotation * (used - fixed)) % max(1, number_of - fixed)
        return jnp.zeros((number_of,), jnp.int32).at[order[jnp.where(places < fixed, places, shifted)]].set(jnp.asarray(tallies, jnp.int32))

    tallies = jnp.where(number % 4 == 0, named(crowded, number // 4), named(ordinary, number - number // 4 - 1))
    mixed = jax.random.permutation(jax.random.fold_in(own, 3), number_of)
    donor, taker = mixed[0:number_of // 2 * 2:2], mixed[1:number_of // 2 * 2:2]
    slack = jnp.minimum(tallies[donor] - 1, most - tallies[taker]) // 2
    slack = jnp.where((donor == order[0]) | (taker == order[0]) | (tallies[taker] == 0), 0, jnp.maximum(slack, 0))
    shifted = jax.random.randint(jax.random.fold_in(own, 4), (number_of // 2,), 0, 1 << 20) % (slack + 1)
    tallies = tallies.at[donor].add(-shifted).at[taker].add(shifted)
    items = jnp.searchsorted(jnp.cumsum(tallies), jnp.arange(rows * top), side="right").astype(jnp.int32)
    grid = items.reshape(top, rows).T
    grid = grid[jax.random.permutation(jax.random.fold_in(own, 1), rows)]
    rotation = jax.random.randint(jax.random.fold_in(own, 2), (rows, 1), 0, top)
    return jnp.take_along_axis(grid, (jnp.arange(top)[None, :] + rotation) % top, axis=1)


def load_shares(amount, total, most, skew, full):
    loads = [(1 << 20) // math.isqrt(rank ** skew) + 1 for rank in range(1, amount + 1)]
    largest = most if full else min(most, max(-(-total // amount), total * loads[0] // sum(loads)))
    least = 1 if total - largest >= amount - 1 else 0
    holding, rest = [largest] + [least] * (amount - 1), total - largest - least * (amount - 1)
    while rest > 0:
        free = [i for i in range(1, amount) if holding[i] < largest] or [i for i in range(1, amount) if holding[i] < most]
        mass, budget = sum([loads[i] for i in free]), rest
        for i in free:
            more = min(most - holding[i], max(1, budget * loads[i] // mass), rest)
            holding[i] = holding[i] + more
            rest = rest - more
    return np.array(holding)


def centred(own_key, shape, scale, bound, shards=(), kind=jnp.bfloat16):
    values = scale * jax.random.normal(own_key, shape, jnp.float32)
    if shards:
        values = values * shard_levels(own_key, shape, shards, -0.22, 0.18)
    return jnp.clip(values, -bound, bound).astype(kind)


def setup_inputs(seed: int = 0) -> dict:
    splits = jax.random.split(jax.random.key(seed), 9)
    scores = centred(splits[0], (COHORTS, VARIANTS, P_SIZE), 1.2, 6.0, ((0, 4), (1, 8)))
    flips = draw_flips(jax.random.fold_in(splits[8], 71), 0)
    presence = with_ends((jax.random.randint(splits[2], (COHORTS, VARIANTS), 0, 8) < 7).astype(jnp.int32), jax.random.fold_in(splits[2], 1), 0, 1)
    covs = draw_covs(jax.random.fold_in(splits[8], 71), 0)
    membership = with_ends((jax.random.randint(splits[4], (MASKS, VARIANTS), 0, 2) < 1).astype(jnp.int32), jax.random.fold_in(splits[4], 1), 0, 1)
    weights = jnp.clip(jnp.exp(math.log(4.0) - 2.7725887 * jax.random.uniform(splits[5], (VARIANTS,), jnp.float32) ** shard_levels(splits[5], (VARIANTS,), ((0, 8),), -0.2, 0.2)), 0.25, 4.0)
    tile_owner_keys = jax.random.split(jax.random.fold_in(splits[6], 1), TILES // TILE_DEV)
    tile_owner_turns = jax.random.permutation(jax.random.fold_in(splits[6], 3), TILES // TILE_DEV)
    tile_owner = jax.vmap(lambda own, number: shared_out(jax.random.fold_in(splits[6], 2), own, number, TILE_DEV, N_GENE, 1, CAP, 2))(tile_owner_keys, tile_owner_turns).reshape((TILES, 1))
    tile_gene = with_ends(jax.random.randint(splits[7], (TILES,), 0, GENE_DEV), jax.random.fold_in(splits[7], 1), 0, GENE_DEV - 1).astype(jnp.int32)
    return {"scores": scores, "flips": flips, "presence": presence, "covs": covs, "membership": membership, "weights": weights, "tile_owner": tile_owner, "tile_gene": tile_gene}


def group_stats(position, scores, flips, presence, covs, membership, weights):
    variant_span = TILE_DEV * VT
    first_row = (position * variant_span).astype(jnp.int32)
    first_tile = (position * TILE_DEV).astype(jnp.int32)
    score_part = lax.dynamic_slice_in_dim(scores, first_row, variant_span, 1).astype(jnp.float32)
    flip_part = lax.dynamic_slice_in_dim(flips, first_row, variant_span, 1).astype(jnp.float32)
    present_part = lax.dynamic_slice_in_dim(presence, first_row, variant_span, 1).astype(jnp.float32)
    cov_part = lax.dynamic_slice_in_dim(covs, first_tile, TILE_DEV, 1).astype(jnp.float32)
    member_part = lax.dynamic_slice_in_dim(membership, first_row, variant_span, 1).astype(jnp.float32)
    weight_part = lax.dynamic_slice_in_dim(weights, first_row, variant_span, 0)
    allele_sign = 1.0 - 2.0 * flip_part
    factor = allele_sign * present_part
    united = lax.optimization_barrier(jnp.sum(score_part * factor[:, :, None], axis=0)).astype(jnp.bfloat16)
    united = lax.optimization_barrier(united)
    tile_sign = allele_sign.reshape(COHORTS, TILE_DEV, VT)
    blocks = lax.optimization_barrier(jnp.sum(tile_sign[:, :, :, None] * tile_sign[:, :, None, :] * cov_part, axis=0)).astype(jnp.bfloat16)
    blocks = lax.optimization_barrier(blocks)
    mask_weights = (weight_part[None, :] * (1.0 + 3.0 * member_part) / 4.0).astype(jnp.bfloat16)
    mask_weights = lax.optimization_barrier(mask_weights)
    w_wide = jnp.transpose(mask_weights.reshape(MASKS, TILE_DEV, VT), (1, 0, 2)).astype(jnp.float32)
    u_wide = united.reshape(TILE_DEV, VT, P_SIZE).astype(jnp.float32)
    w_square = w_wide * w_wide
    tile_burden = jnp.einsum('kmv,kvp->kmp', w_wide, u_wide, precision=lax.Precision.HIGHEST)
    tile_square = jnp.einsum('kmv,kvp->kmp', w_square, u_wide * u_wide, precision=lax.Precision.HIGHEST)
    v_wide = blocks.astype(jnp.float32)
    carried = jnp.einsum('kij,kmj->kmi', v_wide, w_wide, precision=lax.Precision.HIGHEST)
    tile_variance = lax.optimization_barrier(jnp.sum(carried * w_wide, axis=2))
    diagonal = jnp.diagonal(v_wide, axis1=1, axis2=2)
    tile_trace = lax.optimization_barrier(jnp.sum(w_square * diagonal[:, None, :], axis=2))
    squared = jnp.einsum('kij,kmj->kmi', v_wide * v_wide, w_square, precision=lax.Precision.HIGHEST)
    tile_spread = lax.optimization_barrier(jnp.sum(squared * w_square, axis=2))
    return (tile_burden, tile_square, tile_variance, tile_trace, tile_spread)

def reference(scores, flips, presence, covs, membership, weights, tile_owner, tile_gene):

    def one_group(position):
        return group_stats(position, scores, flips, presence, covs, membership, weights)
    results = lax.map(one_group, jnp.arange(N_GENE, dtype=jnp.int32))
    tile_burden, tile_square, tile_variance, tile_trace, tile_spread = [value.reshape((TILES,) + value.shape[2:]) for value in results]
    gene_ids = (tile_owner[:, 0] * GENE_DEV + tile_gene).astype(jnp.int32)
    gene_burden = jax.ops.segment_sum(tile_burden, gene_ids, num_segments=GENES)
    gene_square = jax.ops.segment_sum(tile_square, gene_ids, num_segments=GENES)
    gene_variance = jax.ops.segment_sum(tile_variance, gene_ids, num_segments=GENES)
    gene_trace = jax.ops.segment_sum(tile_trace, gene_ids, num_segments=GENES)
    gene_spread = jax.ops.segment_sum(tile_spread, gene_ids, num_segments=GENES)
    burden_z = gene_burden / jnp.sqrt(jnp.maximum(gene_variance, 1.0))[:, :, None]
    skat_z = (gene_square - gene_trace[:, :, None]) / jnp.sqrt(jnp.maximum(2.0 * gene_spread, 1.0))[:, :, None]
    return (burden_z, skat_z)
```

```python
import functools

import jax
import jax.numpy as jnp
from jax import lax
from jax.experimental import pallas as pl
from jax.experimental.pallas import tpu as pltpu
from jax.sharding import PartitionSpec as P

GENE_DEV = 16
F32 = jnp.float32
BF16 = jnp.bfloat16


def eye_mask(n):
    return lax.broadcasted_iota(jnp.int32, (n, n), 0) == lax.broadcasted_iota(jnp.int32, (n, n), 1)


def upper_mask(n):
    return lax.broadcasted_iota(jnp.int32, (n, n), 0) < lax.broadcasted_iota(jnp.int32, (n, n), 1)


def diagonal_of(row, eye):
    return jnp.where(eye, jnp.broadcast_to(row, eye.shape), 0.0).astype(BF16)


def dot(a, b):
    return jnp.dot(a, b, preferred_element_type=F32)


def split(value):
    high = value.astype(BF16)
    return high, (value - high.astype(F32)).astype(BF16)


def spec(shape, index):
    return pl.BlockSpec(shape, index)


def call(body, name, prefetch, grid, in_specs, out_specs, out_shape, args, scratch=()):
    return pl.pallas_call(
        body,
        name=name,
        grid_spec=pltpu.PrefetchScalarGridSpec(
            num_scalar_prefetch=len(prefetch),
            grid=grid,
            in_specs=in_specs,
            out_specs=out_specs,
            scratch_shapes=list(scratch),
        ),
        out_shape=out_shape,
        compiler_params=pltpu.CompilerParams(vmem_limit_bytes=48 * 1024 * 1024),
    )(*prefetch, *args)


def shaped(shape, dtype):
    return jax.ShapeDtypeStruct(shape, dtype)


class Chunk:
    def __init__(self, start, size, unit, width):
        self.half = size // 2
        self.unit = unit
        self.size = size
        self.steps = self.half // unit
        self.base = start // unit
        self.start = start
        self.rows = self.half * width
        self.block = unit * width


def plan(tile_count, width):
    sizes = [tile_count // 4] * 3 + [tile_count // 6, tile_count // 12]
    chunks, start = [], 0
    for size in sizes:
        unit = size // 2
        while start % unit or unit % 1:
            unit //= 2
        chunks.append(Chunk(start, size, unit, width))
        start += size
    assert start == tile_count
    return chunks


def factor_of(flip_ref, pres_ref, cols):
    return (1.0 - 2.0 * flip_ref[:, cols].astype(F32)) * pres_ref[:, cols].astype(F32)


def sends(ch, width, me, scores, flips, presence):
    quarter = scores.shape[1] // 4

    def body(me_ref, a_ref, b_ref, flip_ref, pres_ref, x_ref, y_ref):
        eye = eye_mask(width)

        def fill(out_ref):
            for t in range(ch.unit):
                rows = slice(t * width, (t + 1) * width)
                diag = diagonal_of(factor_of(flip_ref, pres_ref, rows), eye)
                out_ref[0, rows, :] = dot(diag, a_ref[rows, :]).astype(BF16)
                out_ref[1, rows, :] = dot(diag, b_ref[rows, :]).astype(BF16)

        @pl.when(pl.program_id(0) == 0)
        def _():
            fill(x_ref)

        @pl.when(pl.program_id(0) == 1)
        def _():
            fill(y_ref)

    def row(s, i):
        return ch.base + s * ch.steps + i

    last = ch.steps - 1
    return call(
        body, f"sends_{ch.start}", (me,), (2, ch.steps),
        [
            spec((ch.block, quarter), lambda s, i, me: (row(s, i), me[0] ^ (1 + s))),
            spec((ch.block, quarter), lambda s, i, me: (row(s, i), me[0] ^ 3)),
            spec((1, ch.block), lambda s, i, me: (0, row(s, i))),
            spec((1, ch.block), lambda s, i, me: (0, row(s, i))),
        ],
        [
            spec((2, ch.block, quarter), lambda s, i, me: (0, jnp.where(s == 0, i, last), 0)),
            spec((2, ch.block, quarter), lambda s, i, me: (0, jnp.where(s == 0, 0, i), 0)),
        ],
        [shaped((2, ch.rows, quarter), BF16)] * 2,
        (scores, scores, flips, presence),
    )


def relays(ch, width, me, scores, flips, presence, got_x, got_y):
    quarter = scores.shape[1] // 4

    def body(me_ref, s_ref, flip_ref, pres_ref, gx_ref, gy_ref, x_ref, y_ref):
        eye = eye_mask(width)

        def fill(got_ref, out_ref):
            for t in range(ch.unit):
                rows = slice(t * width, (t + 1) * width)
                diag = diagonal_of(factor_of(flip_ref, pres_ref, rows), eye)
                value = dot(diag, s_ref[rows, :]) + got_ref[0, rows, :].astype(F32)
                out_ref[rows, :] = value.astype(BF16)

        @pl.when(pl.program_id(0) == 0)
        def _():
            fill(gx_ref, x_ref)

        @pl.when(pl.program_id(0) == 1)
        def _():
            fill(gy_ref, y_ref)

    def row(s, i):
        return ch.base + s * ch.steps + i

    last = ch.steps - 1

    def first(s, i):
        return jnp.where(s == 0, i, last)

    def second(s, i):
        return jnp.where(s == 0, 0, i)

    return call(
        body, f"relays_{ch.start}", (me,), (2, ch.steps),
        [
            spec((ch.block, quarter), lambda s, i, me: (row(s, i), me[0] ^ (2 - s))),
            spec((1, ch.block), lambda s, i, me: (0, row(s, i))),
            spec((1, ch.block), lambda s, i, me: (0, row(s, i))),
            spec((1, ch.block, quarter), lambda s, i, me: (1, first(s, i), 0)),
            spec((1, ch.block, quarter), lambda s, i, me: (1, second(s, i), 0)),
        ],
        [
            spec((ch.block, quarter), lambda s, i, me: (first(s, i), 0)),
            spec((ch.block, quarter), lambda s, i, me: (second(s, i), 0)),
        ],
        [shaped((ch.rows, quarter), BF16)] * 2,
        (scores, flips, presence, got_x, got_y),
    )


def weights_of(weight_ref, member_ref, cols):
    return (weight_ref[:, cols] * (1.0 + 3.0 * member_ref[:, cols].astype(F32)) / 4.0).astype(BF16)


def tile_stats(ch, width, me, scores, flips, presence, member, weights, diag_sum, got, relayed):
    quarter = scores.shape[1] // 4
    mask_count = member.shape[0]
    group = diag_sum.shape[0] * 8 // diag_sum.shape[0]

    def body(me_ref, s_ref, flip_ref, pres_ref, member_ref, weight_ref, d_ref,
             gx_ref, gy_ref, rx_ref, ry_ref, burden_ref, diff_ref):
        eye = eye_mask(width)

        def fill(got_ref, relay_ref):
            for t in range(ch.unit):
                rows = slice(t * width, (t + 1) * width)
                diag = diagonal_of(factor_of(flip_ref, pres_ref, rows), eye)
                value = dot(diag, s_ref[rows, :]) + got_ref[0, rows, :].astype(F32)
                united = (value + relay_ref[rows, :].astype(F32)).astype(BF16)
                wide = united.astype(F32)
                w = weights_of(weight_ref, member_ref, rows)
                w_wide = w.astype(F32)
                w_square = w_wide * w_wide
                w_high, w_low = split(w_square)
                w_both = jnp.concatenate([w_high.astype(F32), w_low.astype(F32)], axis=0).astype(BF16)
                s_high, s_low = split(wide * wide)
                square = dot(w_both, s_high) + dot(w_both, s_low)
                square = square[:mask_count] + square[mask_count:]
                tile = t + ch.unit * (pl.program_id(0) * ch.steps + pl.program_id(1))
                trace = jnp.sum(w_square * d_ref[t : t + 1, :], axis=1, keepdims=True)
                burden_ref[t] = dot(w, united)
                diff_ref[t] = square - trace

        @pl.when(pl.program_id(0) == 0)
        def _():
            fill(gx_ref, rx_ref)

        @pl.when(pl.program_id(0) == 1)
        def _():
            fill(gy_ref, ry_ref)

    def row(s, i):
        return ch.base + s * ch.steps + i

    last = ch.steps - 1

    def first(s, i):
        return jnp.where(s == 0, i, last)

    def second(s, i):
        return jnp.where(s == 0, 0, i)

    diag_rows = diag_sum.reshape(-1, ch.unit, width)
    return call(
        body, f"stats_{ch.start}", (me,), (2, ch.steps),
        [
            spec((ch.block, quarter), lambda s, i, me: (row(s, i), me[0])),
            spec((1, ch.block), lambda s, i, me: (0, row(s, i))),
            spec((1, ch.block), lambda s, i, me: (0, row(s, i))),
            spec((mask_count, ch.block), lambda s, i, me: (0, row(s, i))),
            spec((1, ch.block), lambda s, i, me: (0, row(s, i))),
            spec((None, ch.unit, width), lambda s, i, me: (row(s, i), 0, 0)),
            spec((1, ch.block, quarter), lambda s, i, me: (0, first(s, i), 0)),
            spec((1, ch.block, quarter), lambda s, i, me: (0, second(s, i), 0)),
            spec((ch.block, quarter), lambda s, i, me: (first(s, i), 0)),
            spec((ch.block, quarter), lambda s, i, me: (second(s, i), 0)),
        ],
        [spec((ch.unit, mask_count, quarter), lambda s, i, me: (s * ch.steps + i, 0, 0))] * 2,
        [shaped((ch.size, mask_count, quarter), F32)] * 2,
        (scores, flips, presence, member, weights, diag_rows, *got, *relayed),
    )


def cov_sends(me, covs, flips):
    tile_count, width = covs.shape[0], covs.shape[1]
    pairs = tile_count // 16
    tiles = 2 * pairs
    rows = pairs * width

    def body(me_ref, cov_ref, flip_ref, x_ref, y_ref, keep_ref, diag_ref):
        step = pl.program_id(0)
        eye = eye_mask(width)
        upper = upper_mask(width)
        for p in range(pairs):
            sides = []
            for t in (2 * p, 2 * p + 1):
                sign = 1.0 - 2.0 * flip_ref[:, t * width : (t + 1) * width].astype(F32)
                block = cov_ref[t]
                sides.append(dot(diagonal_of(sign, eye), block) * sign)
                row = jnp.sum(jnp.where(eye, block.astype(F32), 0.0), axis=0, keepdims=True)
                diag_ref[0, t : t + 1, :] = row
            folded = jnp.where(upper, sides[0], sides[1]).astype(BF16)
            at = slice(p * width, (p + 1) * width)

            @pl.when(step < 2)
            def _():
                x_ref[0, at, :] = folded

            @pl.when((step >= 2) & (step < 4))
            def _():
                y_ref[0, at, :] = folded

            @pl.when(step >= 4)
            def _():
                keep_ref[0, at, :] = folded

    def block(step, me):
        part = jnp.where(step < 2, 1 + 2 * step, jnp.where(step < 4, step, jnp.where(step < 6, 6 - step, 0)))
        half = jnp.where(step < 2, 0, jnp.where(step < 4, 1, (step - 4) % 2))
        return (me[0] ^ part) * 2 + half

    x_index = lambda s, me: (jnp.minimum(s, 1), 0, 0)
    y_index = lambda s, me: (jnp.clip(s - 2, 0, 1), 0, 0)
    keep_index = lambda s, me: (jnp.clip(s - 4, 0, 3), 0, 0)
    return call(
        body, "cov_sends", (me,), (8,),
        [
            spec((tiles, width, width), lambda s, me: (block(s, me), 0, 0)),
            spec((1, tiles * width), lambda s, me: (0, block(s, me))),
        ],
        [
            spec((1, rows, width), x_index),
            spec((1, rows, width), y_index),
            spec((1, rows, width), keep_index),
            spec((1, tiles, width), lambda s, me: (block(s, me), 0, 0)),
        ],
        [
            shaped((2, rows, width), BF16),
            shaped((2, rows, width), BF16),
            shaped((4, rows, width), BF16),
            shaped((8, tiles, width), F32),
        ],
        (covs, flips),
    )


def cov_relays(keep, got_x, got_y):
    rows, width = keep.shape[1], keep.shape[2]

    def body(kx_ref, ky_ref, gx_ref, gy_ref, x_ref, y_ref):
        x_ref[...] = (kx_ref[0].astype(F32) + gx_ref[0].astype(F32)).astype(BF16)
        y_ref[...] = (ky_ref[0].astype(F32) + gy_ref[0].astype(F32)).astype(BF16)

    def at(i):
        return spec((1, rows, width), lambda s: (i, 0, 0))

    return call(
        body, "cov_relays", (), (1,),
        [at(0), at(1), at(1), at(1)],
        [spec((rows, width), lambda s: (0, 0))] * 2,
        [shaped((rows, width), BF16)] * 2,
        (keep, keep, got_x, got_y),
    )


def moments(me, owner, gene, owner_count, keep, got, relayed, diag_sum, member, weights):
    rows, width = keep.shape[1], keep.shape[2]
    pairs = rows // width
    mask_count = member.shape[0]
    tiles = 4 * pairs

    def body(me_ref, owner_ref, gene_ref, kx_ref, ky_ref, gx_ref, gy_ref, rx_ref, ry_ref,
             d_ref, member_ref, weight_ref, out_ref):
        upper = upper_mask(width)
        lower = jnp.logical_not(upper | eye_mask(width))
        out_ref[...] = jnp.zeros_like(out_ref)
        sub = lax.broadcasted_iota(jnp.int32, (mask_count, GENE_DEV * mask_count), 0)
        lane = lax.broadcasted_iota(jnp.int32, (mask_count, GENE_DEV * mask_count), 1)
        matching = (lane % mask_count) == sub
        lane_gene = lax.broadcasted_iota(jnp.int32, (1, GENE_DEV * mask_count), 1) // mask_count
        for h, (k_ref, g_ref, r_ref) in enumerate(((kx_ref, gx_ref, rx_ref), (ky_ref, gy_ref, ry_ref))):
            for p in range(pairs):
                at = slice(p * width, (p + 1) * width)
                block = k_ref[0, at, :].astype(F32) + g_ref[0, at, :].astype(F32)
                block = block + r_ref[at, :].astype(F32)
                for e, keep_mask in ((0, upper), (1, lower)):
                    t = 2 * (h * pairs + p) + e
                    half = jnp.where(keep_mask, block, 0.0).astype(BF16)
                    wide = half.astype(F32)
                    cols = slice(t * width, (t + 1) * width)
                    w = weights_of(weight_ref, member_ref, cols)
                    w_wide = w.astype(F32)
                    w_square = w_wide * w_wide
                    d = d_ref[h, 2 * p + e : 2 * p + e + 1, :]
                    w_high, w_low = split(w_square)
                    w_both = jnp.concatenate([w_high.astype(F32), w_low.astype(F32)], axis=0).astype(BF16)
                    s_high, s_low = split(wide * wide)
                    squared = dot(w_both, s_high) + dot(w_both, s_low)
                    squared = squared[:mask_count] + squared[mask_count:]
                    variance = jnp.sum(2.0 * dot(w, half) * w_wide + w_square * d, axis=1, keepdims=True)
                    spread = jnp.sum(
                        2.0 * squared * w_square + (w_square * d) * (w_square * d), axis=1, keepdims=True
                    )
                    index = me_ref[0] * tiles + t
                    here = lane_gene == gene_ref[index]
                    for at_row, value in ((0, variance), (owner_count, spread)):
                        line = jnp.sum(jnp.where(matching, value, 0.0), axis=0, keepdims=True)
                        target = pl.ds(owner_ref[index] + at_row, 1)
                        out_ref[target, :] = out_ref[target, :] + jnp.where(here, line, 0.0)

    def at(i):
        return spec((1, rows, width), lambda s, *_: (i, 0, 0))

    flat = spec((rows, width), lambda s, *_: (0, 0))
    return call(
        body, "moments", (me, owner, gene), (1,),
        [
            at(2), at(3), at(0), at(0), flat, flat,
            spec((2, 2 * pairs, width), lambda s, me, *_: (me[0], 0, 0)),
            spec((mask_count, tiles * width), lambda s, me, *_: (0, me[0])),
            spec((1, tiles * width), lambda s, me, *_: (0, me[0])),
        ],
        spec((2 * owner_count, GENE_DEV * mask_count), lambda s, *_: (0, 0)),
        shaped((2 * owner_count, GENE_DEV * mask_count), F32),
        (keep, keep, *got, *relayed, diag_sum, member, weights),
    )


def gene_sums(place, owner, gene, owner_count, moment, stats):
    mask_count, quarter = stats[0][0].shape[1:]
    block = GENE_DEV * mask_count
    extra = 16
    stacks = owner_count // 2
    counts = [burden.shape[0] for burden, _ in stats]

    def body(place_ref, owner_ref, gene_ref, m_ref, *refs):
        tile_refs = refs[: 2 * len(counts)]
        send_ref, keep_ref, b_acc, d_acc = refs[2 * len(counts) :]
        b_acc[...] = jnp.zeros_like(b_acc)
        d_acc[...] = jnp.zeros_like(d_acc)
        t = 0
        for k, count in enumerate(counts):
            for i in range(count):
                where = owner_ref[t] * GENE_DEV + gene_ref[t]
                b_acc[where] = b_acc[where] + tile_refs[2 * k][i]
                d_acc[where] = d_acc[where] + tile_refs[2 * k + 1][i]
                t += 1
        core = place_ref[0] % 2
        stack = place_ref[0] // 2

        def fill(ref, j, other):
            who = 2 * (stack ^ j) + (core ^ other)
            lines = pl.ds(who * GENE_DEV, GENE_DEV)
            ref[j, 0:block, :] = b_acc[lines].reshape(block, quarter).astype(ref.dtype)
            ref[j, block : 2 * block, :] = d_acc[lines].reshape(block, quarter).astype(ref.dtype)
            high_v, low_v = split(m_ref[pl.ds(who, 1), :])
            high_s, low_s = split(m_ref[pl.ds(who + owner_count, 1), :])
            parts = [v.astype(F32) for v in (high_v, low_v, high_s, low_s)]
            parts.append(jnp.zeros((extra - 4, quarter), F32))
            ref[j, 2 * block :, :] = jnp.concatenate(parts, axis=0).astype(ref.dtype)

        for j in range(stacks):
            fill(send_ref, j, 1)
            fill(keep_ref, j, 0)

    lines = 2 * block + extra
    whole = lambda shape: spec(shape, lambda s, *_: (0,) * len(shape))
    flat = [value for pair in stats for value in pair]
    return call(
        body, "gene_sums", (place, owner, gene), (1,),
        [whole(moment.shape)] + [whole(value.shape) for value in flat],
        [whole((stacks, lines, quarter))] * 2,
        [shaped((stacks, lines, quarter), BF16), shaped((stacks, lines, quarter), F32)],
        (moment, *flat),
        scratch=[pltpu.VMEM((owner_count * GENE_DEV, mask_count, quarter), F32)] * 2,
    )


def stack_sums(keep, got):
    stacks, lines, quarter = keep.shape

    def body(keep_ref, got_ref, own_ref, *send_refs):
        own_ref[...] = keep_ref[0] + got_ref[0].astype(F32)
        for j in range(1, stacks):
            send_refs[j - 1][...] = (keep_ref[j] + got_ref[j].astype(F32)).astype(BF16)

    whole = lambda shape: spec(shape, lambda s: (0,) * len(shape))
    return call(
        body, "stack_sums", (), (1,),
        [whole(keep.shape)] * 2,
        [whole((lines, quarter))] * stacks,
        [shaped((lines, quarter), F32)] + [shaped((lines, quarter), BF16)] * (stacks - 1),
        (keep, got),
    )


def finish(own, received, mask_count):
    lines, quarter = own.shape
    block = GENE_DEV * mask_count

    def body(own_ref, *refs):
        got_refs, (burden_ref, skat_ref) = refs[:-2], refs[-2:]
        total = own_ref[...]
        for ref in got_refs:
            total = total + ref[...].astype(F32)
        eye = eye_mask(block)

        def column(first):
            line = total[2 * block + first : 2 * block + first + 1, :]
            line = line + total[2 * block + first + 1 : 2 * block + first + 2, :]
            return jnp.sum(jnp.where(eye, jnp.broadcast_to(line, eye.shape), 0.0), axis=1, keepdims=True)

        burden_ref[...] = total[:block] / jnp.sqrt(jnp.maximum(column(0), 1.0))
        skat_ref[...] = total[block : 2 * block] / jnp.sqrt(jnp.maximum(2.0 * column(2), 1.0))

    whole = lambda shape: spec(shape, lambda s: (0,) * len(shape))
    return call(
        body, "finish", (), (1,),
        [whole(own.shape)] * (1 + len(received)),
        [whole((block, quarter))] * 2,
        [shaped((block, quarter), F32)] * 2,
        (own, *received),
    )


def shards(scores, flips, presence, covs, membership, weights, tile_owner, tile_gene):
    cohort_count = lax.axis_size("cohort")
    owner_count = lax.axis_size("gene")
    assert cohort_count == 4 and owner_count % 2 == 0
    tile_count = tile_gene.shape[0]
    width = covs.shape[-1]
    mask_count = membership.shape[0]
    scores, covs = scores[0], covs[0]
    weights = weights[None, :]
    me = lax.axis_index("cohort").astype(jnp.int32).reshape(1)
    place = lax.axis_index("gene").astype(jnp.int32).reshape(1)
    owner = tile_owner[:, 0]

    def across(value, bit):
        return lax.ppermute(value, "cohort", [(i, i ^ bit) for i in range(cohort_count)])

    def stacked(value, offset):
        return lax.ppermute(value, "gene", [(i, i ^ offset) for i in range(owner_count)])

    chunks = plan(tile_count, width)
    got = {}
    relayed = {}

    def exchange(k):
        x, y = sends(chunks[k], width, me, scores, flips, presence)
        got[k] = (across(x, 1), across(y, 2))

    def forward(k):
        x, y = relays(chunks[k], width, me, scores, flips, presence, *got[k])
        relayed[k] = (across(x, 2), across(y, 1))

    exchange(0)
    cov_x, cov_y, cov_keep, diag = cov_sends(me, covs, flips)
    cov_got = (across(cov_x, 1), across(cov_y, 2))
    diag_sum = diag + across(diag, 1)
    diag_sum = diag_sum + across(diag_sum, 2)
    exchange(1)
    forward(0)
    cov_relay_x, cov_relay_y = cov_relays(cov_keep, *cov_got)
    cov_relayed = (across(cov_relay_x, 2), across(cov_relay_y, 1))
    exchange(2)
    forward(1)
    moment = moments(
        me, owner, tile_gene, owner_count, cov_keep, cov_got, cov_relayed, diag_sum, membership, weights
    )
    moment = moment + across(moment, 1)
    moment = moment + across(moment, 2)
    for k in range(3, len(chunks)):
        exchange(k)
        forward(k - 1)
    forward(len(chunks) - 1)
    stats = [
        tile_stats(
            ch, width, me, scores, flips, presence, membership, weights, diag_sum, got[k], relayed[k]
        )
        for k, ch in enumerate(chunks)
    ]
    send, keep = gene_sums(place, owner, tile_gene, owner_count, moment, stats)
    own, *onward = stack_sums(keep, stacked(send, 1))
    received = [stacked(value, 2 * (j + 1)) for j, value in enumerate(onward)]
    burden_z, skat_z = finish(own, received, mask_count)
    shape = (GENE_DEV, mask_count, burden_z.shape[-1])
    return burden_z.reshape(shape), skat_z.reshape(shape)


def solution(mesh):
    return jax.shard_map(
        shards,
        mesh=mesh,
        in_specs=(
            P("cohort", "gene", None),
            P("cohort", "gene"),
            P("cohort", "gene"),
            P("cohort", "gene", None, None),
            P(None, "gene"),
            P("gene"),
            P("gene", None),
            P("gene"),
        ),
        out_specs=(P("gene", None, "cohort"), P("gene", None, "cohort")),
        check_vma=False,
    )
```
